32 devices in a mesh: dp: 8 (over z, x), row: 4 (over y, core).
Axes of the slice: x: 2, y: 2, z: 4, core: 2. Of those that a mesh axis runs over, the one named last changes fastest.
Arguments:
- queries: bfloat16 [2048, 4096], P('dp', 'row'), may hold values from -100 to 100
- passages: bfloat16 [2048, 4096], P('dp', 'row'), may hold values from -10 to 10
- cached: bfloat16 [16384, 4096], P('dp', 'row'), may hold values from -6 to 6
- hard_shard: int32 [2048, 4], P('dp'), may hold values from 0 to 7, as said below
- hard_row: int32 [2048, 4], P('dp'), may hold values from 0 to 2047
- query_source: int32 [2048], P('dp'), may hold values from 0 to 7
- block_source: int32 [16], replicated, may hold values from 0 to 7
Outputs:
- mean_loss: float32 [], replicated
- query_grad: bfloat16 [2048, 4096], P('dp', 'row')
- passage_grad: bfloat16 [2048, 4096], P('dp', 'row')
The draws below stay inside these ranges and needn't reach their ends.
Inputs may be any that keep to these rules, and one draw needn't show every extreme that they name: `hard_shard`: one cache shard, drawn with the seed, is named exactly 256 times among the 256 queries of every device; among one device's queries no shard is named more than 256 times, and the other shards share the rest as evenly as possible; a query's 4 hard negatives lie in 4 different shards.
All inputs are finite; a program needn't handle non-finite values.
Results may differ from the reference program's by a relative error of at most 0.0043.
Values may be sent and summed in bfloat16 or wider, within the bound.
A program may use at most 128 MiB of HBM per device.

```python
import math
import jax
import jax.numpy as jnp
from jax import lax

D = 4096
ROWS = 256
CD = 2048
H = 4
BLOCK = 128
NSRC = 8
NQ = 2048
NP = 2048
NC = 16384
NB = 16


def cache_rows(key, indices):
    cache_key = jax.random.fold_in(key, 31)

    def one_row(index):
        row_key = jax.random.fold_in(cache_key, index)
        return jnp.clip(jax.random.normal(row_key, (D,), jnp.float32), -6.0, 6.0)
    return jax.vmap(one_row)(indices)


def hard_indices(key):
    index_key = jax.random.fold_in(key, 47)
    hot_key, order_key, row_key = jax.random.split(index_key, 3)
    n_data = NQ // ROWS
    capacity = min(ROWS, 3 * ROWS * H // n_data)
    hottest = jax.random.randint(hot_key, (), 0, n_data, dtype=jnp.int32)
    hard_slots = jnp.arange(H, dtype=jnp.int32)

    def one_block(block_key):
        first_key, second_key = jax.random.split(block_key)
        placed = jax.random.permutation(first_key, ROWS).astype(jnp.int32)[:, None]
        others = jax.random.permutation(second_key, n_data - 1).astype(jnp.int32)
        early = placed < capacity
        counter = placed * H + hard_slots[None, :] - jnp.minimum(placed, capacity) - early.astype(jnp.int32)
        counter = jnp.maximum(counter, 0)
        other_shard = (hottest + 1 + others[counter % (n_data - 1)]) % n_data
        is_hot = early & (hard_slots[None, :] == 0)
        return jnp.where(is_hot, hottest, other_shard).astype(jnp.int32)
    block_keys = jax.random.split(order_key, n_data)
    shard_ids = jax.vmap(one_block)(block_keys).reshape(NQ, H)
    row_ids = jax.random.randint(row_key, (NQ, H), 0, CD, dtype=jnp.int32)
    return (shard_ids, row_ids)


def passage_base(key):
    own_key, topic_key, share_key = jax.random.split(jax.random.fold_in(key, 11), 3)
    topic_count = NP // 16
    own_part = jnp.clip(jax.random.normal(own_key, (NP, D), jnp.float32), -6.0, 6.0)
    topic_part = jnp.clip(jax.random.normal(topic_key, (topic_count, D), jnp.float32), -6.0, 6.0)
    shares = jax.random.uniform(share_key, (topic_count, 1), jnp.float32, 0.3, 0.8)
    members = jnp.tile(topic_part, (16, 1))
    member_share = jnp.tile(shares, (16, 1))
    values = jnp.sqrt(1.0 - member_share) * own_part + jnp.sqrt(member_share) * members
    return values


def draw_passages(key, part):
    return passage_base(key).astype(jnp.bfloat16)


def draw_cached(key, part):
    return cache_rows(key, jnp.arange(NC, dtype=jnp.int32)).astype(jnp.bfloat16)


def draw_hard_shard(key, part):
    return hard_indices(key)[0]


def draw_hard_row(key, part):
    return hard_indices(key)[1]


def draw_queries(key, part):
    own_key, match_key, pull_key = jax.random.split(jax.random.fold_in(key, 23), 3)
    passage_values = passage_base(key)
    shard_ids, row_ids = hard_indices(key)
    root_width = math.sqrt(D)
    match_scale = jnp.exp(jax.random.uniform(match_key, (NQ, 1), jnp.float32, math.log(5.0), math.log(14.0))) / root_width
    pull_scale = jnp.exp(jax.random.uniform(pull_key, (NQ, H), jnp.float32, math.log(4.0), math.log(13.0))) / root_width
    values = jnp.clip(jax.random.normal(own_key, (NQ, D), jnp.float32), -6.0, 6.0) + match_scale * passage_values
    for hard_slot in range(H):
        flat_index = (shard_ids[:, hard_slot] * CD + row_ids[:, hard_slot]).astype(jnp.int32)
        values = values + pull_scale[:, hard_slot:hard_slot + 1] * cache_rows(key, flat_index)
    return values.astype(jnp.bfloat16)


def place_ends(array, rng, low, largest):
    index_at = [jax.random.randint(jax.random.fold_in(rng, axis), (), 0, length) for axis, length in enumerate(array.shape)]
    widest = array.shape.index(max(array.shape))
    next_to = index_at[:widest] + [(index_at[widest] + 1) % array.shape[widest]] + index_at[widest + 1:]
    return array.at[tuple(index_at)].set(low).at[tuple(next_to)].set(largest)


def setup_inputs(seed: int = 0) -> dict:
    splits = jax.random.split(jax.random.key(seed), 8)
    return {
        "queries": draw_queries(jax.random.fold_in(splits[7], 71), 0),
        "passages": draw_passages(jax.random.fold_in(splits[7], 71), 0),
        "cached": draw_cached(jax.random.fold_in(splits[7], 71), 0),
        "hard_shard": draw_hard_shard(jax.random.fold_in(splits[7], 71), 0),
        "hard_row": draw_hard_row(jax.random.fold_in(splits[7], 71), 0),
        "query_source": place_ends(jax.random.randint(splits[5], (NQ,), 0, NSRC), jax.random.fold_in(splits[5], 1), 0, NSRC - 1).astype(jnp.int32),
        "block_source": place_ends(jax.random.randint(splits[6], (NB,), 0, NSRC), jax.random.fold_in(splits[6], 1), 0, NSRC - 1).astype(jnp.int32),
    }


NEG_FILL = -1e+30

def reference(queries, passages, cached, hard_shard, hard_row, query_source, block_source):
    logit_scale = 1.0 / math.sqrt(D)
    logits = logit_scale * jnp.dot(queries, passages.T, preferred_element_type=jnp.float32)
    cache_index = (hard_shard * CD + hard_row).astype(jnp.int32)
    hard_rows = jnp.take(cached, cache_index.reshape(-1), axis=0).reshape(NQ, H, D)
    hard_logits = logit_scale * jnp.einsum('qd,qhd->qh', queries.astype(jnp.float32), hard_rows.astype(jnp.float32))
    columns = jnp.arange(NP, dtype=jnp.int32)
    targets = jnp.arange(NQ, dtype=jnp.int32)
    column_source = jnp.repeat(block_source, BLOCK)
    positive = columns[None, :] == targets[:, None]
    allowed = (query_source[:, None] != column_source[None, :]) | positive
    masked = jnp.where(allowed, logits, NEG_FILL)
    maximum = jnp.maximum(lax.optimization_barrier(jnp.max(masked, axis=1)), lax.optimization_barrier(jnp.max(hard_logits, axis=1)))
    exponent = jnp.exp(masked - maximum[:, None])
    hard_expo = jnp.exp(hard_logits - maximum[:, None])
    totals = lax.optimization_barrier(jnp.sum(exponent, axis=1)) + lax.optimization_barrier(jnp.sum(hard_expo, axis=1))
    pos_logit = lax.optimization_barrier(jnp.sum(jnp.where(positive, logits, 0.0), axis=1))
    per_query = maximum + jnp.log(totals) - pos_logit
    mean_loss = jnp.sum(per_query) / NQ
    weights = (exponent / totals[:, None] - positive.astype(jnp.float32)).astype(jnp.bfloat16)
    hard_weights = (hard_expo / totals[:, None]).astype(jnp.bfloat16)
    query_grad = jnp.dot(weights, passages, preferred_element_type=jnp.float32)
    query_grad = query_grad + jnp.einsum('qh,qhd->qd', hard_weights.astype(jnp.float32), hard_rows.astype(jnp.float32))
    passage_grad = jnp.dot(weights.T, queries, preferred_element_type=jnp.float32)
    return (mean_loss, query_grad.astype(jnp.bfloat16), passage_grad.astype(jnp.bfloat16))
```

```python
import functools
import math

import jax
import jax.numpy as jnp
from jax import lax
from jax.experimental import pallas as pl
from jax.experimental.pallas import tpu as pltpu
from jax.sharding import PartitionSpec as P

D = 4096
BLOCK = 128
LANES = 128
NEG_FILL = -1e30
MESH = pl.DeviceIdType.MESH


def fetch_hard(cached, hard_shard, hard_row, n_data):
    row_count, hard_count = hard_shard.shape
    width_dev = cached.shape[1]
    capacity = min(row_count, 3 * row_count * hard_count // n_data)
    owners = hard_shard.reshape(-1)
    wanted = hard_row.reshape(-1)
    one_hot = (owners[:, None] == jnp.arange(n_data, dtype=jnp.int32)[None, :]).astype(jnp.int32)
    before = jnp.cumsum(one_hot, axis=0) - one_hot
    slot_index = jnp.sum(before * one_hot, axis=1)
    target = owners * capacity + slot_index
    requests = (
        jnp.zeros((n_data * capacity,), jnp.int32).at[target].set(wanted).reshape(n_data, capacity)
    )
    asked_rows = lax.all_to_all(requests, "dp", split_axis=0, concat_axis=0, tiled=True)
    picked = jnp.take(cached, asked_rows.reshape(-1), axis=0, mode="clip")
    picked = picked.reshape(asked_rows.shape[0], asked_rows.shape[1], width_dev)
    replies = lax.all_to_all(picked, "dp", split_axis=0, concat_axis=0, tiled=True)
    reply_rows = replies.reshape(n_data * capacity, width_dev)
    hard_rows = [
        jnp.take(reply_rows, target.reshape(row_count, hard_count)[:, h], axis=0, mode="clip")
        for h in range(hard_count)
    ]
    return hard_rows


def gather_kernel(n, n_row, q_ref, p_ref, pall, qall, lsum, lpart, lrecv,
                  gsend, grecv, lsend, lrecv_sem, own_sem):
    me = lax.axis_index("dp")
    r = lax.axis_index("row")
    lines = n // 2
    a = me // 2
    b = me % 2
    rows = q_ref.shape[0]
    part = rows // n_row
    across = a * 2 + 1 - b

    barrier = pltpu.get_barrier_semaphore()
    pl.semaphore_signal(barrier, inc=1, device_id=(across, r), device_id_type=MESH)
    for k in range(1, n_row):
        pl.semaphore_signal(
            barrier, inc=1, device_id=(me, lax.rem(r + k, n_row)), device_id_type=MESH
        )

    @pl.when(a < lines - 1)
    def _():
        pl.semaphore_signal(barrier, inc=1, device_id=(me + 2, r), device_id_type=MESH)

    @pl.when(a > 0)
    def _():
        pl.semaphore_signal(barrier, inc=1, device_id=(me - 2, r), device_id_type=MESH)

    neighbours = (a < lines - 1).astype(jnp.int32) + (a > 0).astype(jnp.int32)
    pl.semaphore_wait(barrier, n_row + neighbours)

    alls = (pall, qall)
    own = (p_ref, q_ref)

    def copy(t, kind, blk, first=False):
        to = (across, me + 2, me - 2)[kind]
        return pltpu.make_async_remote_copy(
            src_ref=own[t] if first else alls[t].at[blk],
            dst_ref=alls[t].at[blk],
            send_sem=gsend.at[t, kind, blk],
            recv_sem=grecv.at[t, blk],
            device_id=(to, r),
            device_id_type=MESH,
        )

    def arrived(t, blk):
        copy(t, 0, blk).wait_recv()

    def start_own(t):
        @pl.when(a < lines - 1)
        def _():
            copy(t, 1, me, True).start()

        @pl.when(a > 0)
        def _():
            copy(t, 2, me, True).start()

        copy(t, 0, me, True).start()

    def multiply(blk, block):
        lpart[blk] = lax.dot_general(
            q_ref[...], block, (((1,), (1,)), ((), ())), preferred_element_type=jnp.float32
        )

    def ship(blk):
        for k in range(1, n_row):
            to = lax.rem(r + k, n_row)
            ship_copy(blk, to, k).start()

    def ship_copy(blk, to, k):
        return pltpu.make_async_remote_copy(
            src_ref=lpart.at[blk, pl.ds(pl.multiple_of(to * part, part), part), :],
            dst_ref=lrecv.at[k - 1, blk],
            send_sem=lsend.at[k - 1, blk],
            recv_sem=lrecv_sem.at[k - 1, blk],
            device_id=(me, to),
            device_id_type=MESH,
        )

    def relay(t, s):
        lo = me - 2 * (s + 1)
        hi = me + 2 * (s + 1)

        @pl.when(lo >= 0)
        def _():
            arrived(t, lo)

            @pl.when(a < lines - 1)
            def _():
                copy(t, 1, lo).start()

            copy(t, 0, lo).start()

        @pl.when(hi < n)
        def _():
            arrived(t, hi)

            @pl.when(a > 0)
            def _():
                copy(t, 2, hi).start()

            copy(t, 0, hi).start()

    def logits_of(s):
        lo = me - 2 * (s + 1)
        hi = me + 2 * (s + 1)
        flip = 1 - 2 * b

        @pl.when(lo >= 0)
        def _():
            multiply(lo, pall[lo])

        @pl.when(hi < n)
        def _():
            multiply(hi, pall[hi])

        @pl.when(lo >= 0)
        def _():
            ship(lo)
            arrived(0, lo + flip)
            multiply(lo + flip, pall[lo + flip])

        @pl.when(hi < n)
        def _():
            ship(hi)
            arrived(0, hi + flip)
            multiply(hi + flip, pall[hi + flip])

        @pl.when(lo >= 0)
        def _():
            ship(lo + flip)

        @pl.when(hi < n)
        def _():
            ship(hi + flip)

    start_own(0)
    own_p = pltpu.make_async_copy(p_ref, pall.at[me], own_sem.at[0])
    own_q = pltpu.make_async_copy(q_ref, qall.at[me], own_sem.at[1])
    own_p.start()
    own_q.start()
    multiply(me, p_ref[...])
    for s in range(lines - 1):
        relay(0, s)
        if s == lines - 2:
            start_own(1)
        if s == 0:
            ship(me)
            arrived(0, across)
            multiply(across, pall[across])
            ship(across)
        else:
            logits_of(s - 1)
    for s in range(lines - 1):
        relay(1, s)
        if s == 0:
            logits_of(lines - 2)
    arrived(1, across)
    flip = 1 - 2 * b
    for s in range(lines - 1):
        lo = me - 2 * (s + 1)
        hi = me + 2 * (s + 1)

        @pl.when(lo >= 0)
        def _():
            arrived(1, lo + flip)

        @pl.when(hi < n)
        def _():
            arrived(1, hi + flip)

    base = pl.multiple_of(r * part, part)
    columns = p_ref.shape[0]
    for blk in range(n):
        total = lpart[blk, pl.ds(base, part), :]
        for k in range(1, n_row):
            ship_copy(blk, lax.rem(r + k, n_row), k).wait_recv()
            total = total + lrecv[k - 1, blk]
        lsum[:, blk * columns:(blk + 1) * columns] = total

    own_p.wait()
    own_q.wait()
    for blk in range(n):
        for k in range(1, n_row):
            ship_copy(blk, lax.rem(r + k, n_row), k).wait_send()
    for t in range(2):
        copy(t, 0, me, True).wait_send()

        @pl.when(a < lines - 1)
        def _():
            copy(t, 1, me, True).wait_send()

        @pl.when(a > 0)
        def _():
            copy(t, 2, me, True).wait_send()

        for s in range(lines - 1):
            lo = me - 2 * (s + 1)
            hi = me + 2 * (s + 1)

            @pl.when(lo >= 0)
            def _():
                copy(t, 0, lo).wait_send()

                @pl.when(a < lines - 1)
                def _():
                    copy(t, 1, lo).wait_send()

            @pl.when(hi < n)
            def _():
                copy(t, 0, hi).wait_send()

                @pl.when(a > 0)
                def _():
                    copy(t, 2, hi).wait_send()


def gather_and_logits(queries, passages, n, n_row):
    rows, width = queries.shape
    prows = passages.shape[0]
    part = rows // n_row
    vmem = pl.BlockSpec(memory_space=pltpu.VMEM)
    return pl.pallas_call(
        functools.partial(gather_kernel, n, n_row),
        name="gather_logits",
        out_shape=(
            jax.ShapeDtypeStruct((n, prows, width), passages.dtype),
            jax.ShapeDtypeStruct((n, rows, width), queries.dtype),
            jax.ShapeDtypeStruct((part, n * prows), jnp.float32),
        ),
        in_specs=[vmem, vmem],
        out_specs=(vmem, vmem, vmem),
        scratch_shapes=[
            pltpu.VMEM((n, rows, prows), jnp.float32),
            pltpu.VMEM((n_row - 1, n, part, prows), jnp.float32),
            pltpu.SemaphoreType.DMA((2, 3, n)),
            pltpu.SemaphoreType.DMA((2, n)),
            pltpu.SemaphoreType.DMA((n_row - 1, n)),
            pltpu.SemaphoreType.DMA((n_row - 1, n)),
            pltpu.SemaphoreType.DMA((2,)),
        ],
        compiler_params=pltpu.CompilerParams(
            collective_id=0, has_side_effects=True, vmem_limit_bytes=56 * 2**20
        ),
    )(queries, passages)


def weights_kernel(n, n_row, columns, w_ref, wrow, wcol, dsend, drecv, rsend, rrecv, csend, crecv,
                   own_sem):
    me = lax.axis_index("dp")
    r = lax.axis_index("row")
    barrier = pltpu.get_barrier_semaphore()
    for j in range(1, n):
        pl.semaphore_signal(
            barrier, inc=1, device_id=(lax.rem(me + j, n), r), device_id_type=MESH
        )
    for k in range(1, n_row):
        pl.semaphore_signal(
            barrier, inc=1, device_id=(me, lax.rem(r + k, n_row)), device_id_type=MESH
        )
    pl.semaphore_wait(barrier, n + n_row - 2)

    def across(j):
        to = lax.rem(me + j, n)
        return pltpu.make_async_remote_copy(
            src_ref=w_ref.at[:, pl.ds(pl.multiple_of(to * columns, columns), columns)],
            dst_ref=wcol.at[r, me],
            send_sem=dsend.at[j - 1],
            recv_sem=drecv.at[j - 1],
            device_id=(to, r),
            device_id_type=MESH,
        )

    def along(k):
        return pltpu.make_async_remote_copy(
            src_ref=w_ref,
            dst_ref=wrow.at[r],
            send_sem=rsend.at[k - 1],
            recv_sem=rrecv.at[k - 1],
            device_id=(me, lax.rem(r + k, n_row)),
            device_id_type=MESH,
        )

    def spread(k):
        return pltpu.make_async_remote_copy(
            src_ref=wcol.at[r],
            dst_ref=wcol.at[r],
            send_sem=csend.at[k - 1],
            recv_sem=crecv.at[k - 1],
            device_id=(me, lax.rem(r + k, n_row)),
            device_id_type=MESH,
        )

    for j in range(1, n):
        across(j).start()
    for k in range(1, n_row):
        along(k).start()
    own_row = pltpu.make_async_copy(w_ref, wrow.at[r], own_sem.at[0])
    own_col = pltpu.make_async_copy(
        w_ref.at[:, pl.ds(pl.multiple_of(me * columns, columns), columns)],
        wcol.at[r, me],
        own_sem.at[1],
    )
    own_row.start()
    own_col.start()
    own_col.wait()
    for j in range(1, n):
        across(j).wait_recv()
    for k in range(1, n_row):
        spread(k).start()
    own_row.wait()
    for k in range(1, n_row):
        along(k).wait_recv()
        spread(k).wait_recv()
    for j in range(1, n):
        across(j).wait_send()
    for k in range(1, n_row):
        along(k).wait_send()
        spread(k).wait_send()


def exchange_weights(weights_ext, n, n_row, columns):
    part, wide = weights_ext.shape
    vmem = pl.BlockSpec(memory_space=pltpu.VMEM)
    dma = pltpu.SemaphoreType.DMA
    return pl.pallas_call(
        functools.partial(weights_kernel, n, n_row, columns),
        name="exchange_weights",
        out_shape=(
            jax.ShapeDtypeStruct((n_row, part, wide), weights_ext.dtype),
            jax.ShapeDtypeStruct((n_row, n, part, columns), weights_ext.dtype),
        ),
        in_specs=[vmem],
        out_specs=(vmem, vmem),
        scratch_shapes=[
            dma((n - 1,)), dma((n - 1,)), dma((n_row - 1,)), dma((n_row - 1,)),
            dma((n_row - 1,)), dma((n_row - 1,)), dma((2,)),
        ],
        compiler_params=pltpu.CompilerParams(collective_id=1, has_side_effects=True),
    )(weights_ext)


def softmax_rows(summed, summed_hard, sources, block_source, first_row, logit_scale):
    logits = logit_scale * summed
    hard_logits = logit_scale * summed_hard
    columns = jnp.arange(logits.shape[1], dtype=jnp.int32)
    targets = first_row + jnp.arange(logits.shape[0], dtype=jnp.int32)
    column_source = jnp.repeat(block_source, BLOCK)
    positive = columns[None, :] == targets[:, None]
    allowed = (sources[:, None] != column_source[None, :]) | positive
    masked = jnp.where(allowed, logits, NEG_FILL)
    maximum = jnp.maximum(jnp.max(masked, axis=1), jnp.max(hard_logits, axis=1))
    exponent = jnp.exp(masked - maximum[:, None])
    hard_expo = jnp.exp(hard_logits - maximum[:, None])
    totals = jnp.sum(exponent, axis=1) + jnp.sum(hard_expo, axis=1)
    pos_logit = jnp.sum(jnp.where(positive, logits, 0.0), axis=1)
    per_query = maximum + jnp.log(totals) - pos_logit
    weights = (exponent / totals[:, None] - positive.astype(jnp.float32)).astype(jnp.bfloat16)
    hard_weights = (hard_expo / totals[:, None]).astype(jnp.bfloat16)
    return (weights, hard_weights, jnp.sum(per_query))


def on_device(queries, passages, cached, hard_shard, hard_row, query_source, block_source):
    row_count, width = queries.shape
    columns = passages.shape[0]
    n_data = lax.axis_size("dp")
    n_row = lax.axis_size("row")
    part = row_count // n_row
    logit_scale = 1.0 / math.sqrt(D)
    hard_rows = fetch_hard(cached, hard_shard, hard_row, n_data)
    hard_count = len(hard_rows)
    pall, qall, summed = gather_and_logits(queries, passages, n_data, n_row)
    q32 = queries.astype(jnp.float32)
    partial_hard = jnp.stack(
        [jnp.sum(q32 * rows.astype(jnp.float32), axis=1) for rows in hard_rows], axis=1
    )
    summed_hard = lax.psum(partial_hard, "row")
    row_at = lax.axis_index("row") * part
    first_row = lax.axis_index("dp") * row_count + row_at
    my_hard = lax.dynamic_slice_in_dim(summed_hard, row_at, part, 0)
    my_source = lax.dynamic_slice_in_dim(query_source, row_at, part, 0)
    weights, hard_weights, local_loss = softmax_rows(
        summed, my_hard, my_source, block_source, first_row, logit_scale
    )
    n_all = weights.shape[1]
    ext = jnp.concatenate(
        [weights, jnp.pad(hard_weights, ((0, 0), (0, LANES - hard_count)))], axis=1
    )
    wrow, wcol = exchange_weights(ext, n_data, n_row, columns)
    loss_sum = lax.psum(local_loss, ("dp", "row"))
    mean_loss = loss_sum / (row_count * n_data)
    wrow = wrow.reshape(row_count, n_all + LANES)
    query_grad = jnp.dot(
        wrow[:, :n_all], pall.reshape(n_data * columns, width), preferred_element_type=jnp.float32
    )
    for h in range(hard_count):
        query_grad = query_grad + wrow[:, n_all + h:n_all + h + 1].astype(
            jnp.float32
        ) * hard_rows[h].astype(jnp.float32)
    passage_grad = lax.dot_general(
        wcol.reshape(n_row, n_data, part, columns),
        qall.reshape(n_data, n_row, part, width).transpose(1, 0, 2, 3),
        (((0, 1, 2), (0, 1, 2)), ((), ())),
        preferred_element_type=jnp.float32,
    )
    return (mean_loss, query_grad.astype(jnp.bfloat16), passage_grad.astype(jnp.bfloat16))


def solution(mesh):
    in_specs = (
        P("dp", "row"),
        P("dp", "row"),
        P("dp", "row"),
        P("dp", None),
        P("dp", None),
        P("dp"),
        P(),
    )
    out_specs = (P(), P("dp", "row"), P("dp", "row"))
    return jax.shard_map(
        on_device, mesh=mesh, in_specs=in_specs, out_specs=out_specs, check_vma=False
    )
```

```python
import functools
import math

import jax
import jax.numpy as jnp
from jax import lax
from jax.experimental import pallas as pl
from jax.experimental.pallas import tpu as pltpu
from jax.sharding import PartitionSpec as P

D = 4096
BLOCK = 128
LANES = 128
NEG_FILL = -1e30
MESH = pl.DeviceIdType.MESH


def fetch_hard(cached, hard_shard, hard_row, n_data):
    row_count, hard_count = hard_shard.shape
    width_dev = cached.shape[1]
    capacity = min(row_count, 3 * row_count * hard_count // n_data)
    owners = hard_shard.reshape(-1)
    wanted = hard_row.reshape(-1)
    one_hot = (owners[:, None] == jnp.arange(n_data, dtype=jnp.int32)[None, :]).astype(jnp.int32)
    before = jnp.cumsum(one_hot, axis=0) - one_hot
    slot_index = jnp.sum(before * one_hot, axis=1)
    target = owners * capacity + slot_index
    requests = (
        jnp.zeros((n_data * capacity,), jnp.int32).at[target].set(wanted).reshape(n_data, capacity)
    )
    asked_rows = lax.all_to_all(requests, "dp", split_axis=0, concat_axis=0, tiled=True)
    picked = jnp.take(cached, asked_rows.reshape(-1), axis=0, mode="clip")
    picked = picked.reshape(asked_rows.shape[0], asked_rows.shape[1], width_dev)
    replies = lax.all_to_all(picked, "dp", split_axis=0, concat_axis=0, tiled=True)
    reply_rows = replies.reshape(n_data * capacity, width_dev)
    by_slot = target.reshape(row_count, hard_count).T.reshape(-1)
    hard_rows = jnp.take(reply_rows, by_slot, axis=0, mode="clip")
    return hard_rows.reshape(hard_count, row_count, width_dev)


def gather_kernel(n, n_row, q_ref, p_ref, pall, qall, lsum, lpart, lrecv,
                  gsend, grecv, lsend, lrecv_sem, own_sem):
    me = lax.axis_index("dp")
    r = lax.axis_index("row")
    lines = n // 2
    a = me // 2
    b = me % 2
    rows = q_ref.shape[0]
    part = rows // n_row
    across = a * 2 + 1 - b

    barrier = pltpu.get_barrier_semaphore()
    pl.semaphore_signal(barrier, inc=1, device_id=(across, r), device_id_type=MESH)
    for k in range(1, n_row):
        pl.semaphore_signal(
            barrier, inc=1, device_id=(me, lax.rem(r + k, n_row)), device_id_type=MESH
        )

    @pl.when(a < lines - 1)
    def _():
        pl.semaphore_signal(barrier, inc=1, device_id=(me + 2, r), device_id_type=MESH)

    @pl.when(a > 0)
    def _():
        pl.semaphore_signal(barrier, inc=1, device_id=(me - 2, r), device_id_type=MESH)

    neighbours = (a < lines - 1).astype(jnp.int32) + (a > 0).astype(jnp.int32)
    pl.semaphore_wait(barrier, n_row + neighbours)

    alls = (pall, qall)
    own = (p_ref, q_ref)

    def copy(t, kind, blk, first=False):
        to = (across, me + 2, me - 2)[kind]
        return pltpu.make_async_remote_copy(
            src_ref=own[t] if first else alls[t].at[blk],
            dst_ref=alls[t].at[blk],
            send_sem=gsend.at[t, kind, blk],
            recv_sem=grecv.at[t, blk],
            device_id=(to, r),
            device_id_type=MESH,
        )

    def arrived(t, blk):
        copy(t, 0, blk).wait_recv()

    def start_own(t):
        @pl.when(a < lines - 1)
        def _():
            copy(t, 1, me, True).start()

        @pl.when(a > 0)
        def _():
            copy(t, 2, me, True).start()

        copy(t, 0, me, True).start()

    def multiply(blk, block):
        lpart[blk] = lax.dot_general(
            q_ref[...], block, (((1,), (1,)), ((), ())), preferred_element_type=jnp.float32
        )

    def ship(blk):
        for k in range(1, n_row):
            to = lax.rem(r + k, n_row)
            ship_copy(blk, to, k).start()

    def ship_copy(blk, to, k):
        return pltpu.make_async_remote_copy(
            src_ref=lpart.at[blk, pl.ds(pl.multiple_of(to * part, part), part), :],
            dst_ref=lrecv.at[k - 1, blk],
            send_sem=lsend.at[k - 1, blk],
            recv_sem=lrecv_sem.at[k - 1, blk],
            device_id=(me, to),
            device_id_type=MESH,
        )

    def relay(t, s):
        lo = me - 2 * (s + 1)
        hi = me + 2 * (s + 1)

        @pl.when(lo >= 0)
        def _():
            arrived(t, lo)

            @pl.when(a < lines - 1)
            def _():
                copy(t, 1, lo).start()

            copy(t, 0, lo).start()

        @pl.when(hi < n)
        def _():
            arrived(t, hi)

            @pl.when(a > 0)
            def _():
                copy(t, 2, hi).start()

            copy(t, 0, hi).start()

    def logits_of(s):
        lo = me - 2 * (s + 1)
        hi = me + 2 * (s + 1)
        flip = 1 - 2 * b

        @pl.when(lo >= 0)
        def _():
            multiply(lo, pall[lo])

        @pl.when(hi < n)
        def _():
            multiply(hi, pall[hi])

        @pl.when(lo >= 0)
        def _():
            ship(lo)
            arrived(0, lo + flip)
            multiply(lo + flip, pall[lo + flip])

        @pl.when(hi < n)
        def _():
            ship(hi)
            arrived(0, hi + flip)
            multiply(hi + flip, pall[hi + flip])

        @pl.when(lo >= 0)
        def _():
            ship(lo + flip)

        @pl.when(hi < n)
        def _():
            ship(hi + flip)

    start_own(0)
    own_p = pltpu.make_async_copy(p_ref, pall.at[me], own_sem.at[0])
    own_q = pltpu.make_async_copy(q_ref, qall.at[me], own_sem.at[1])
    own_p.start()
    own_q.start()
    multiply(me, p_ref[...])
    for s in range(lines - 1):
        relay(0, s)
        if s == lines - 2:
            start_own(1)
        if s == 0:
            ship(me)
            arrived(0, across)
            multiply(across, pall[across])
            ship(across)
        else:
            logits_of(s - 1)
    for s in range(lines - 1):
        relay(1, s)
        if s == 0:
            logits_of(lines - 2)
    arrived(1, across)
    flip = 1 - 2 * b
    for s in range(lines - 1):
        lo = me - 2 * (s + 1)
        hi = me + 2 * (s + 1)

        @pl.when(lo >= 0)
        def _():
            arrived(1, lo + flip)

        @pl.when(hi < n)
        def _():
            arrived(1, hi + flip)

    base = pl.multiple_of(r * part, part)
    columns = p_ref.shape[0]
    for blk in range(n):
        total = lpart[blk, pl.ds(base, part), :]
        for k in range(1, n_row):
            ship_copy(blk, lax.rem(r + k, n_row), k).wait_recv()
            total = total + lrecv[k - 1, blk]
        lsum[:, blk * columns:(blk + 1) * columns] = total

    own_p.wait()
    own_q.wait()
    for blk in range(n):
        for k in range(1, n_row):
            ship_copy(blk, lax.rem(r + k, n_row), k).wait_send()
    for t in range(2):
        copy(t, 0, me, True).wait_send()

        @pl.when(a < lines - 1)
        def _():
            copy(t, 1, me, True).wait_send()

        @pl.when(a > 0)
        def _():
            copy(t, 2, me, True).wait_send()

        for s in range(lines - 1):
            lo = me - 2 * (s + 1)
            hi = me + 2 * (s + 1)

            @pl.when(lo >= 0)
            def _():
                copy(t, 0, lo).wait_send()

                @pl.when(a < lines - 1)
                def _():
                    copy(t, 1, lo).wait_send()

            @pl.when(hi < n)
            def _():
                copy(t, 0, hi).wait_send()

                @pl.when(a > 0)
                def _():
                    copy(t, 2, hi).wait_send()


def gather_and_logits(queries, passages, n, n_row):
    rows, width = queries.shape
    prows = passages.shape[0]
    part = rows // n_row
    vmem = pl.BlockSpec(memory_space=pltpu.VMEM)
    return pl.pallas_call(
        functools.partial(gather_kernel, n, n_row),
        name="gather_logits",
        out_shape=(
            jax.ShapeDtypeStruct((n, prows, width), passages.dtype),
            jax.ShapeDtypeStruct((n, rows, width), queries.dtype),
            jax.ShapeDtypeStruct((part, n * prows), jnp.float32),
        ),
        in_specs=[vmem, vmem],
        out_specs=(vmem, vmem, vmem),
        scratch_shapes=[
            pltpu.VMEM((n, rows, prows), jnp.float32),
            pltpu.VMEM((n_row - 1, n, part, prows), jnp.float32),
            pltpu.SemaphoreType.DMA((2, 3, n)),
            pltpu.SemaphoreType.DMA((2, n)),
            pltpu.SemaphoreType.DMA((n_row - 1, n)),
            pltpu.SemaphoreType.DMA((n_row - 1, n)),
            pltpu.SemaphoreType.DMA((2,)),
        ],
        compiler_params=pltpu.CompilerParams(
            collective_id=0, has_side_effects=True, vmem_limit_bytes=56 * 2**20
        ),
    )(queries, passages)


def weights_kernel(n, n_row, columns, w_ref, loss_ref, wrow, wcol, table, dsend, drecv, tsend,
                   trecv, rsend, rrecv, own_sem):
    me = lax.axis_index("dp")
    r = lax.axis_index("row")
    n_line = n_row // 2
    y = r // 2
    core = r % 2
    partner = y * 2 + 1 - core
    barrier = pltpu.get_barrier_semaphore()
    for j in range(1, n):
        pl.semaphore_signal(
            barrier, inc=1, device_id=(lax.rem(me + j, n), r), device_id_type=MESH
        )
    for k in range(1, n_line):
        pl.semaphore_signal(
            barrier, inc=1, device_id=(me, lax.rem(r + 2 * k, n_row)), device_id_type=MESH
        )
    pl.semaphore_signal(barrier, inc=1, device_id=(me, partner), device_id_type=MESH)
    pl.semaphore_wait(barrier, n + n_line - 1)

    def across(j):
        to = lax.rem(me + j, n)
        return pltpu.make_async_remote_copy(
            src_ref=w_ref.at[:, pl.ds(pl.multiple_of(to * columns, columns), columns)],
            dst_ref=wcol.at[y, core, me],
            send_sem=dsend.at[j - 1],
            recv_sem=drecv.at[j - 1],
            device_id=(to, r),
            device_id_type=MESH,
        )

    def tell(j):
        return pltpu.make_async_remote_copy(
            src_ref=loss_ref,
            dst_ref=table.at[y, core, me],
            send_sem=tsend.at[j - 1],
            recv_sem=trecv.at[j - 1],
            device_id=(lax.rem(me + j, n), r),
            device_id_type=MESH,
        )

    def along(which, k):
        out = (wrow, wcol, table)[which]
        return pltpu.make_async_remote_copy(
            src_ref=w_ref if which == 0 else out.at[y, core],
            dst_ref=out.at[y, core],
            send_sem=rsend.at[which, k - 1],
            recv_sem=rrecv.at[which, k - 1],
            device_id=(me, lax.rem(r + 2 * k, n_row)),
            device_id_type=MESH,
        )

    def beside(which):
        out = (wrow, wcol, table)[which]
        return pltpu.make_async_remote_copy(
            src_ref=out.at[:, core],
            dst_ref=out.at[:, core],
            send_sem=rsend.at[which, n_line - 1],
            recv_sem=rrecv.at[which, n_line - 1],
            device_id=(me, partner),
            device_id_type=MESH,
        )

    for j in range(1, n):
        across(j).start()
        tell(j).start()
    for k in range(1, n_line):
        along(0, k).start()
    owns = (
        pltpu.make_async_copy(w_ref, wrow.at[y, core], own_sem.at[0]),
        pltpu.make_async_copy(
            w_ref.at[:, pl.ds(pl.multiple_of(me * columns, columns), columns)],
            wcol.at[y, core, me],
            own_sem.at[1],
        ),
        pltpu.make_async_copy(loss_ref, table.at[y, core, me], own_sem.at[2]),
    )
    for own in owns:
        own.start()
    for own in owns:
        own.wait()
    for j in range(1, n):
        across(j).wait_recv()
        tell(j).wait_recv()
    for k in range(1, n_line):
        along(1, k).start()
        along(2, k).start()
    for which in range(3):
        for k in range(1, n_line):
            along(which, k).wait_recv()
        beside(which).start()
    for which in range(3):
        beside(which).wait_recv()
    for j in range(1, n):
        across(j).wait_send()
        tell(j).wait_send()
    for which in range(3):
        for k in range(1, n_line):
            along(which, k).wait_send()
        beside(which).wait_send()


def exchange_weights(weights_ext, loss_tile, n, n_row, columns):
    part, wide = weights_ext.shape
    vmem = pl.BlockSpec(memory_space=pltpu.VMEM)
    dma = pltpu.SemaphoreType.DMA
    n_line = n_row // 2
    return pl.pallas_call(
        functools.partial(weights_kernel, n, n_row, columns),
        name="exchange_weights",
        out_shape=(
            jax.ShapeDtypeStruct((n_line, 2, part, wide), weights_ext.dtype),
            jax.ShapeDtypeStruct((n_line, 2, n, part, columns), weights_ext.dtype),
            jax.ShapeDtypeStruct((n_line, 2, n) + loss_tile.shape, loss_tile.dtype),
        ),
        in_specs=[vmem, vmem],
        out_specs=(vmem, vmem, vmem),
        scratch_shapes=[
            dma((n - 1,)), dma((n - 1,)), dma((n - 1,)), dma((n - 1,)),
            dma((3, n_line)), dma((3, n_line)), dma((3,)),
        ],
        compiler_params=pltpu.CompilerParams(collective_id=1, has_side_effects=True),
    )(weights_ext, loss_tile)


def hard_kernel(n_row, x_ref, out, send, recv, own_sem):
    me = lax.axis_index("dp")
    r = lax.axis_index("row")
    barrier = pltpu.get_barrier_semaphore()
    for k in range(1, n_row):
        pl.semaphore_signal(
            barrier, inc=1, device_id=(me, lax.rem(r + k, n_row)), device_id_type=MESH
        )
    pl.semaphore_wait(barrier, n_row - 1)

    def along(k):
        return pltpu.make_async_remote_copy(
            src_ref=x_ref,
            dst_ref=out.at[r],
            send_sem=send.at[k - 1],
            recv_sem=recv.at[k - 1],
            device_id=(me, lax.rem(r + k, n_row)),
            device_id_type=MESH,
        )

    for k in range(1, n_row):
        along(k).start()
    own = pltpu.make_async_copy(x_ref, out.at[r], own_sem)
    own.start()
    own.wait()
    for k in range(1, n_row):
        along(k).wait()


def gather_hard(partial_hard, n_row):
    vmem = pl.BlockSpec(memory_space=pltpu.VMEM)
    dma = pltpu.SemaphoreType.DMA
    return pl.pallas_call(
        functools.partial(hard_kernel, n_row),
        name="gather_hard",
        out_shape=jax.ShapeDtypeStruct((n_row,) + partial_hard.shape, partial_hard.dtype),
        in_specs=[vmem],
        out_specs=vmem,
        scratch_shapes=[dma((n_row - 1,)), dma((n_row - 1,)), dma(())],
        compiler_params=pltpu.CompilerParams(collective_id=2, has_side_effects=True),
    )(partial_hard)


def softmax_rows(summed, summed_hard, sources, block_source, first_row, logit_scale):
    logits = logit_scale * summed
    hard_logits = logit_scale * summed_hard
    columns = jnp.arange(logits.shape[1], dtype=jnp.int32)
    targets = first_row + jnp.arange(logits.shape[0], dtype=jnp.int32)
    column_source = jnp.repeat(block_source, BLOCK)
    positive = columns[None, :] == targets[:, None]
    allowed = (sources[:, None] != column_source[None, :]) | positive
    masked = jnp.where(allowed, logits, NEG_FILL)
    maximum = jnp.maximum(jnp.max(masked, axis=1), jnp.max(hard_logits, axis=1))
    exponent = jnp.exp(masked - maximum[:, None])
    hard_expo = jnp.exp(hard_logits - maximum[:, None])
    totals = jnp.sum(exponent, axis=1) + jnp.sum(hard_expo, axis=1)
    pos_logit = jnp.sum(jnp.where(positive, logits, 0.0), axis=1)
    per_query = maximum + jnp.log(totals) - pos_logit
    weights = (exponent / totals[:, None] - positive.astype(jnp.float32)).astype(jnp.bfloat16)
    hard_weights = (hard_expo / totals[:, None]).astype(jnp.bfloat16)
    return (weights, hard_weights, jnp.sum(per_query))


def on_device(queries, passages, cached, hard_shard, hard_row, query_source, block_source):
    row_count, width = queries.shape
    columns = passages.shape[0]
    n_data = lax.axis_size("dp")
    n_row = lax.axis_size("row")
    part = row_count // n_row
    logit_scale = 1.0 / math.sqrt(D)
    hard_rows = fetch_hard(cached, hard_shard, hard_row, n_data)
    hard_count = hard_rows.shape[0]
    pall, qall, summed = gather_and_logits(queries, passages, n_data, n_row)
    partial_hard = jnp.sum(
        queries.astype(jnp.float32)[None] * hard_rows.astype(jnp.float32), axis=2
    )
    partial_hard = jnp.pad(partial_hard, ((0, -hard_count % 8), (0, 0)))
    summed_hard = jnp.sum(gather_hard(partial_hard, n_row), axis=0)[:hard_count]
    row_at = lax.axis_index("row") * part
    first_row = lax.axis_index("dp") * row_count + row_at
    my_hard = lax.dynamic_slice_in_dim(summed_hard, row_at, part, 1).T
    my_source = lax.dynamic_slice_in_dim(query_source, row_at, part, 0)
    weights, hard_weights, local_loss = softmax_rows(
        summed, my_hard, my_source, block_source, first_row, logit_scale
    )
    n_all = weights.shape[1]
    ext = jnp.concatenate(
        [weights, jnp.pad(hard_weights, ((0, 0), (0, LANES - hard_count)))], axis=1
    )
    loss_tile = jnp.full((8, LANES), local_loss, jnp.float32)
    wrow, wcol, losses = exchange_weights(ext, loss_tile, n_data, n_row, columns)
    loss_sum = jnp.sum(losses[:, :, :, 0, 0])
    mean_loss = loss_sum / (row_count * n_data)
    wrow = wrow.reshape(row_count, n_all + LANES)
    query_grad = jnp.dot(
        wrow[:, :n_all], pall.reshape(n_data * columns, width), preferred_element_type=jnp.float32
    )
    for h in range(hard_count):
        query_grad = query_grad + wrow[:, n_all + h:n_all + h + 1].astype(
            jnp.float32
        ) * hard_rows[h].astype(jnp.float32)
    passage_grad = lax.dot_general(
        wcol.reshape(n_row, n_data, part, columns),
        qall.reshape(n_data, n_row, part, width).transpose(1, 0, 2, 3),
        (((0, 1, 2), (0, 1, 2)), ((), ())),
        preferred_element_type=jnp.float32,
    )
    return (mean_loss, query_grad.astype(jnp.bfloat16), passage_grad.astype(jnp.bfloat16))


def solution(mesh):
    in_specs = (
        P("dp", "row"),
        P("dp", "row"),
        P("dp", "row"),
        P("dp", None),
        P("dp", None),
        P("dp"),
        P(),
    )
    out_specs = (P(), P("dp", "row"), P("dp", "row"))
    return jax.shard_map(
        on_device, mesh=mesh, in_specs=in_specs, out_specs=out_specs, check_vma=False
    )
```

```python
import functools
import math

import jax
import jax.numpy as jnp
from jax import lax
from jax.experimental import pallas as pl
from jax.experimental.pallas import tpu as pltpu
from jax.sharding import PartitionSpec as P

D = 4096
BLOCK = 128
LANES = 128
NEG_FILL = -1e30
MESH = pl.DeviceIdType.MESH


def spill_kernel(n, hot, rows_ref, out, send, recv, own_sem):
    me = lax.axis_index("dp")
    r = lax.axis_index("row")
    barrier = pltpu.get_barrier_semaphore()

    def copy(j):
        to = (hot + j) % n
        return pltpu.make_async_remote_copy(
            src_ref=rows_ref.at[to],
            dst_ref=out,
            send_sem=send.at[j - 1],
            recv_sem=recv,
            device_id=(to, r),
            device_id_type=MESH,
        )

    @pl.when(me == hot)
    def _():
        for j in range(1, n):
            pl.semaphore_signal(
                barrier, inc=1, device_id=((hot + j) % n, r), device_id_type=MESH
            )

    @pl.when(me != hot)
    def _():
        pl.semaphore_signal(barrier, inc=1, device_id=(hot, r), device_id_type=MESH)

    pl.semaphore_wait(barrier, 1 + (me == hot).astype(jnp.int32) * (n - 2))

    @pl.when(me == hot)
    def _():
        for j in range(1, n):
            copy(j).start()
        own = pltpu.make_async_copy(rows_ref.at[hot], out, own_sem)
        own.start()
        own.wait()
        for j in range(1, n):
            copy(j).wait_send()

    @pl.when(me != hot)
    def _():
        copy(1).wait_recv()


def spill(n, hot, rows):
    vmem = pl.BlockSpec(memory_space=pltpu.VMEM)
    dma = pltpu.SemaphoreType.DMA
    return pl.pallas_call(
        functools.partial(spill_kernel, n, hot),
        name=f"spill_{hot}",
        out_shape=jax.ShapeDtypeStruct(rows.shape[1:], rows.dtype),
        in_specs=[vmem],
        out_specs=vmem,
        scratch_shapes=[dma((n - 1,)), dma(()), dma(())],
        compiler_params=pltpu.CompilerParams(collective_id=3 + hot, has_side_effects=True),
    )(rows)


def fetch_hard(cached, hard_shard, hard_row, n_data):
    row_count, hard_count = hard_shard.shape
    width_dev = cached.shape[1]
    capacity = min(row_count, 3 * row_count * hard_count // n_data)
    others = -(-(row_count * hard_count - capacity) // (n_data - 1))
    common = min(capacity - 16, -(-others // 16) * 16)
    owners = hard_shard.reshape(-1)
    wanted = hard_row.reshape(-1)
    one_hot = (owners[:, None] == jnp.arange(n_data, dtype=jnp.int32)[None, :]).astype(jnp.int32)
    before = jnp.cumsum(one_hot, axis=0) - one_hot
    slot_index = jnp.sum(before * one_hot, axis=1)
    hot = jnp.argmax(jnp.sum(one_hot, axis=0)).astype(jnp.int32)
    target = owners * capacity + slot_index
    requests = (
        jnp.zeros((n_data * capacity,), jnp.int32).at[target].set(wanted).reshape(n_data, capacity)
    )
    asked_rows = lax.all_to_all(requests, "dp", split_axis=0, concat_axis=0, tiled=True)
    picked = jnp.take(cached, asked_rows[:, :common].reshape(-1), axis=0, mode="clip")
    picked = picked.reshape(n_data, common, width_dev)
    replies = lax.all_to_all(picked, "dp", split_axis=0, concat_axis=0, tiled=True)
    extra = jnp.take(cached, asked_rows[:, common:].reshape(-1), axis=0, mode="clip")
    extra = extra.reshape(n_data, capacity - common, width_dev)
    spilled = lax.switch(hot, [functools.partial(spill, n_data, k) for k in range(n_data)], extra)
    reply_rows = jnp.concatenate([replies.reshape(n_data * common, width_dev), spilled], axis=0)
    place = jnp.where(
        slot_index < common, owners * common + slot_index, n_data * common + slot_index - common
    )
    by_slot = place.reshape(row_count, hard_count).T.reshape(-1)
    hard_rows = jnp.take(reply_rows, by_slot, axis=0, mode="clip")
    return hard_rows.reshape(hard_count, row_count, width_dev)


def gather_kernel(n, n_row, q_ref, p_ref, pall, qall, lsum, lpart, lrecv,
                  gsend, grecv, lsend, lrecv_sem, own_sem):
    me = lax.axis_index("dp")
    r = lax.axis_index("row")
    lines = n // 2
    a = me // 2
    b = me % 2
    rows = q_ref.shape[0]
    part = rows // n_row
    across = a * 2 + 1 - b

    barrier = pltpu.get_barrier_semaphore()
    pl.semaphore_signal(barrier, inc=1, device_id=(across, r), device_id_type=MESH)
    for k in range(1, n_row):
        pl.semaphore_signal(
            barrier, inc=1, device_id=(me, lax.rem(r + k, n_row)), device_id_type=MESH
        )

    @pl.when(a < lines - 1)
    def _():
        pl.semaphore_signal(barrier, inc=1, device_id=(me + 2, r), device_id_type=MESH)

    @pl.when(a > 0)
    def _():
        pl.semaphore_signal(barrier, inc=1, device_id=(me - 2, r), device_id_type=MESH)

    neighbours = (a < lines - 1).astype(jnp.int32) + (a > 0).astype(jnp.int32)
    pl.semaphore_wait(barrier, n_row + neighbours)

    alls = (pall, qall)
    own = (p_ref, q_ref)

    def copy(t, kind, blk, first=False):
        to = (across, me + 2, me - 2)[kind]
        return pltpu.make_async_remote_copy(
            src_ref=own[t] if first else alls[t].at[blk],
            dst_ref=alls[t].at[blk],
            send_sem=gsend.at[t, kind, blk],
            recv_sem=grecv.at[t, blk],
            device_id=(to, r),
            device_id_type=MESH,
        )

    def arrived(t, blk):
        copy(t, 0, blk).wait_recv()

    def start_own(t):
        @pl.when(a < lines - 1)
        def _():
            copy(t, 1, me, True).start()

        @pl.when(a > 0)
        def _():
            copy(t, 2, me, True).start()

        copy(t, 0, me, True).start()

    def multiply(blk, block):
        lpart[blk] = lax.dot_general(
            q_ref[...], block, (((1,), (1,)), ((), ())), preferred_element_type=jnp.float32
        )

    def ship(blk):
        for k in range(1, n_row):
            to = lax.rem(r + k, n_row)
            ship_copy(blk, to, k).start()

    def ship_copy(blk, to, k):
        return pltpu.make_async_remote_copy(
            src_ref=lpart.at[blk, pl.ds(pl.multiple_of(to * part, part), part), :],
            dst_ref=lrecv.at[k - 1, blk],
            send_sem=lsend.at[k - 1, blk],
            recv_sem=lrecv_sem.at[k - 1, blk],
            device_id=(me, to),
            device_id_type=MESH,
        )

    def relay(t, s):
        lo = me - 2 * (s + 1)
        hi = me + 2 * (s + 1)

        @pl.when(lo >= 0)
        def _():
            arrived(t, lo)

            @pl.when(a < lines - 1)
            def _():
                copy(t, 1, lo).start()

            copy(t, 0, lo).start()

        @pl.when(hi < n)
        def _():
            arrived(t, hi)

            @pl.when(a > 0)
            def _():
                copy(t, 2, hi).start()

            copy(t, 0, hi).start()

    def logits_of(s):
        lo = me - 2 * (s + 1)
        hi = me + 2 * (s + 1)
        flip = 1 - 2 * b

        @pl.when(lo >= 0)
        def _():
            multiply(lo, pall[lo])

        @pl.when(hi < n)
        def _():
            multiply(hi, pall[hi])

        @pl.when(lo >= 0)
        def _():
            ship(lo)
            arrived(0, lo + flip)
            multiply(lo + flip, pall[lo + flip])

        @pl.when(hi < n)
        def _():
            ship(hi)
            arrived(0, hi + flip)
            multiply(hi + flip, pall[hi + flip])

        @pl.when(lo >= 0)
        def _():
            ship(lo + flip)

        @pl.when(hi < n)
        def _():
            ship(hi + flip)

    start_own(0)
    own_p = pltpu.make_async_copy(p_ref, pall.at[me], own_sem.at[0])
    own_q = pltpu.make_async_copy(q_ref, qall.at[me], own_sem.at[1])
    own_p.start()
    own_q.start()
    multiply(me, p_ref[...])
    for s in range(lines - 1):
        relay(0, s)
        if s == lines - 2:
            start_own(1)
        if s == 0:
            ship(me)
            arrived(0, across)
            multiply(across, pall[across])
            ship(across)
        else:
            logits_of(s - 1)
    for s in range(lines - 1):
        relay(1, s)
        if s == 0:
            logits_of(lines - 2)
    arrived(1, across)
    flip = 1 - 2 * b
    for s in range(lines - 1):
        lo = me - 2 * (s + 1)
        hi = me + 2 * (s + 1)

        @pl.when(lo >= 0)
        def _():
            arrived(1, lo + flip)

        @pl.when(hi < n)
        def _():
            arrived(1, hi + flip)

    base = pl.multiple_of(r * part, part)
    columns = p_ref.shape[0]
    for blk in range(n):
        total = lpart[blk, pl.ds(base, part), :]
        for k in range(1, n_row):
            ship_copy(blk, lax.rem(r + k, n_row), k).wait_recv()
            total = total + lrecv[k - 1, blk]
        lsum[:, blk * columns:(blk + 1) * columns] = total

    own_p.wait()
    own_q.wait()
    for blk in range(n):
        for k in range(1, n_row):
            ship_copy(blk, lax.rem(r + k, n_row), k).wait_send()
    for t in range(2):
        copy(t, 0, me, True).wait_send()

        @pl.when(a < lines - 1)
        def _():
            copy(t, 1, me, True).wait_send()

        @pl.when(a > 0)
        def _():
            copy(t, 2, me, True).wait_send()

        for s in range(lines - 1):
            lo = me - 2 * (s + 1)
            hi = me + 2 * (s + 1)

            @pl.when(lo >= 0)
            def _():
                copy(t, 0, lo).wait_send()

                @pl.when(a < lines - 1)
                def _():
                    copy(t, 1, lo).wait_send()

            @pl.when(hi < n)
            def _():
                copy(t, 0, hi).wait_send()

                @pl.when(a > 0)
                def _():
                    copy(t, 2, hi).wait_send()


def gather_and_logits(queries, passages, n, n_row):
    rows, width = queries.shape
    prows = passages.shape[0]
    part = rows // n_row
    vmem = pl.BlockSpec(memory_space=pltpu.VMEM)
    return pl.pallas_call(
        functools.partial(gather_kernel, n, n_row),
        name="gather_logits",
        out_shape=(
            jax.ShapeDtypeStruct((n, prows, width), passages.dtype),
            jax.ShapeDtypeStruct((n, rows, width), queries.dtype),
            jax.ShapeDtypeStruct((part, n * prows), jnp.float32),
        ),
        in_specs=[vmem, vmem],
        out_specs=(vmem, vmem, vmem),
        scratch_shapes=[
            pltpu.VMEM((n, rows, prows), jnp.float32),
            pltpu.VMEM((n_row - 1, n, part, prows), jnp.float32),
            pltpu.SemaphoreType.DMA((2, 3, n)),
            pltpu.SemaphoreType.DMA((2, n)),
            pltpu.SemaphoreType.DMA((n_row - 1, n)),
            pltpu.SemaphoreType.DMA((n_row - 1, n)),
            pltpu.SemaphoreType.DMA((2,)),
        ],
        compiler_params=pltpu.CompilerParams(
            collective_id=0, has_side_effects=True, vmem_limit_bytes=56 * 2**20
        ),
    )(queries, passages)


def weights_kernel(n, n_row, columns, w_ref, loss_ref, wrow, wcol, table, dsend, drecv, tsend,
                   trecv, rsend, rrecv, own_sem):
    me = lax.axis_index("dp")
    r = lax.axis_index("row")
    n_line = n_row // 2
    y = r // 2
    core = r % 2
    partner = y * 2 + 1 - core
    barrier = pltpu.get_barrier_semaphore()
    for j in range(1, n):
        pl.semaphore_signal(
            barrier, inc=1, device_id=(lax.rem(me + j, n), r), device_id_type=MESH
        )
    for k in range(1, n_line):
        pl.semaphore_signal(
            barrier, inc=1, device_id=(me, lax.rem(r + 2 * k, n_row)), device_id_type=MESH
        )
    pl.semaphore_signal(barrier, inc=1, device_id=(me, partner), device_id_type=MESH)
    pl.semaphore_wait(barrier, n + n_line - 1)

    def across(j):
        to = lax.rem(me + j, n)
        return pltpu.make_async_remote_copy(
            src_ref=w_ref.at[:, pl.ds(pl.multiple_of(to * columns, columns), columns)],
            dst_ref=wcol.at[y, core, me],
            send_sem=dsend.at[j - 1],
            recv_sem=drecv.at[j - 1],
            device_id=(to, r),
            device_id_type=MESH,
        )

    def tell(j):
        return pltpu.make_async_remote_copy(
            src_ref=loss_ref,
            dst_ref=table.at[y, core, me],
            send_sem=tsend.at[j - 1],
            recv_sem=trecv.at[j - 1],
            device_id=(lax.rem(me + j, n), r),
            device_id_type=MESH,
        )

    def along(which, k):
        out = (wrow, wcol, table)[which]
        return pltpu.make_async_remote_copy(
            src_ref=w_ref if which == 0 else out.at[y, core],
            dst_ref=out.at[y, core],
            send_sem=rsend.at[which, k - 1],
            recv_sem=rrecv.at[which, k - 1],
            device_id=(me, lax.rem(r + 2 * k, n_row)),
            device_id_type=MESH,
        )

    def beside(which):
        out = (wrow, wcol, table)[which]
        return pltpu.make_async_remote_copy(
            src_ref=out.at[:, core],
            dst_ref=out.at[:, core],
            send_sem=rsend.at[which, n_line - 1],
            recv_sem=rrecv.at[which, n_line - 1],
            device_id=(me, partner),
            device_id_type=MESH,
        )

    for j in range(1, n):
        across(j).start()
        tell(j).start()
    for k in range(1, n_line):
        along(0, k).start()
    owns = (
        pltpu.make_async_copy(w_ref, wrow.at[y, core], own_sem.at[0]),
        pltpu.make_async_copy(
            w_ref.at[:, pl.ds(pl.multiple_of(me * columns, columns), columns)],
            wcol.at[y, core, me],
            own_sem.at[1],
        ),
        pltpu.make_async_copy(loss_ref, table.at[y, core, me], own_sem.at[2]),
    )
    for own in owns:
        own.start()
    for own in owns:
        own.wait()
    for j in range(1, n):
        across(j).wait_recv()
        tell(j).wait_recv()
    for k in range(1, n_line):
        along(1, k).start()
        along(2, k).start()
    for which in range(3):
        for k in range(1, n_line):
            along(which, k).wait_recv()
        beside(which).start()
    for which in range(3):
        beside(which).wait_recv()
    for j in range(1, n):
        across(j).wait_send()
        tell(j).wait_send()
    for which in range(3):
        for k in range(1, n_line):
            along(which, k).wait_send()
        beside(which).wait_send()


def exchange_weights(weights_ext, loss_tile, n, n_row, columns):
    part, wide = weights_ext.shape
    vmem = pl.BlockSpec(memory_space=pltpu.VMEM)
    dma = pltpu.SemaphoreType.DMA
    n_line = n_row // 2
    return pl.pallas_call(
        functools.partial(weights_kernel, n, n_row, columns),
        name="exchange_weights",
        out_shape=(
            jax.ShapeDtypeStruct((n_line, 2, part, wide), weights_ext.dtype),
            jax.ShapeDtypeStruct((n_line, 2, n, part, columns), weights_ext.dtype),
            jax.ShapeDtypeStruct((n_line, 2, n) + loss_tile.shape, loss_tile.dtype),
        ),
        in_specs=[vmem, vmem],
        out_specs=(vmem, vmem, vmem),
        scratch_shapes=[
            dma((n - 1,)), dma((n - 1,)), dma((n - 1,)), dma((n - 1,)),
            dma((3, n_line)), dma((3, n_line)), dma((3,)),
        ],
        compiler_params=pltpu.CompilerParams(collective_id=1, has_side_effects=True),
    )(weights_ext, loss_tile)


def hard_kernel(n_row, x_ref, out, send, recv, own_sem):
    me = lax.axis_index("dp")
    r = lax.axis_index("row")
    barrier = pltpu.get_barrier_semaphore()
    for k in range(1, n_row):
        pl.semaphore_signal(
            barrier, inc=1, device_id=(me, lax.rem(r + k, n_row)), device_id_type=MESH
        )
    pl.semaphore_wait(barrier, n_row - 1)

    def along(k):
        return pltpu.make_async_remote_copy(
            src_ref=x_ref,
            dst_ref=out.at[r],
            send_sem=send.at[k - 1],
            recv_sem=recv.at[k - 1],
            device_id=(me, lax.rem(r + k, n_row)),
            device_id_type=MESH,
        )

    for k in range(1, n_row):
        along(k).start()
    own = pltpu.make_async_copy(x_ref, out.at[r], own_sem)
    own.start()
    own.wait()
    for k in range(1, n_row):
        along(k).wait()


def gather_hard(partial_hard, n_row):
    vmem = pl.BlockSpec(memory_space=pltpu.VMEM)
    dma = pltpu.SemaphoreType.DMA
    return pl.pallas_call(
        functools.partial(hard_kernel, n_row),
        name="gather_hard",
        out_shape=jax.ShapeDtypeStruct((n_row,) + partial_hard.shape, partial_hard.dtype),
        in_specs=[vmem],
        out_specs=vmem,
        scratch_shapes=[dma((n_row - 1,)), dma((n_row - 1,)), dma(())],
        compiler_params=pltpu.CompilerParams(collective_id=2, has_side_effects=True),
    )(partial_hard)


def softmax_rows(summed, summed_hard, sources, block_source, first_row, logit_scale):
    logits = logit_scale * summed
    hard_logits = logit_scale * summed_hard
    columns = jnp.arange(logits.shape[1], dtype=jnp.int32)
    targets = first_row + jnp.arange(logits.shape[0], dtype=jnp.int32)
    column_source = jnp.repeat(block_source, BLOCK)
    positive = columns[None, :] == targets[:, None]
    allowed = (sources[:, None] != column_source[None, :]) | positive
    masked = jnp.where(allowed, logits, NEG_FILL)
    maximum = jnp.maximum(jnp.max(masked, axis=1), jnp.max(hard_logits, axis=1))
    exponent = jnp.exp(masked - maximum[:, None])
    hard_expo = jnp.exp(hard_logits - maximum[:, None])
    totals = jnp.sum(exponent, axis=1) + jnp.sum(hard_expo, axis=1)
    pos_logit = jnp.sum(jnp.where(positive, logits, 0.0), axis=1)
    per_query = maximum + jnp.log(totals) - pos_logit
    weights = (exponent / totals[:, None] - positive.astype(jnp.float32)).astype(jnp.bfloat16)
    hard_weights = (hard_expo / totals[:, None]).astype(jnp.bfloat16)
    return (weights, hard_weights, jnp.sum(per_query))


def on_device(queries, passages, cached, hard_shard, hard_row, query_source, block_source):
    row_count, width = queries.shape
    columns = passages.shape[0]
    n_data = lax.axis_size("dp")
    n_row = lax.axis_size("row")
    part = row_count // n_row
    logit_scale = 1.0 / math.sqrt(D)
    hard_rows = fetch_hard(cached, hard_shard, hard_row, n_data)
    hard_count = hard_rows.shape[0]
    pall, qall, summed = gather_and_logits(queries, passages, n_data, n_row)
    partial_hard = jnp.sum(
        queries.astype(jnp.float32)[None] * hard_rows.astype(jnp.float32), axis=2
    )
    partial_hard = jnp.pad(partial_hard, ((0, -hard_count % 8), (0, 0)))
    summed_hard = jnp.sum(gather_hard(partial_hard, n_row), axis=0)[:hard_count]
    row_at = lax.axis_index("row") * part
    first_row = lax.axis_index("dp") * row_count + row_at
    my_hard = lax.dynamic_slice_in_dim(summed_hard, row_at, part, 1).T
    my_source = lax.dynamic_slice_in_dim(query_source, row_at, part, 0)
    weights, hard_weights, local_loss = softmax_rows(
        summed, my_hard, my_source, block_source, first_row, logit_scale
    )
    n_all = weights.shape[1]
    ext = jnp.concatenate(
        [weights, jnp.pad(hard_weights, ((0, 0), (0, LANES - hard_count)))], axis=1
    )
    loss_tile = jnp.full((8, LANES), local_loss, jnp.float32)
    wrow, wcol, losses = exchange_weights(ext, loss_tile, n_data, n_row, columns)
    loss_sum = jnp.sum(losses[:, :, :, 0, 0])
    mean_loss = loss_sum / (row_count * n_data)
    wrow = wrow.reshape(row_count, n_all + LANES)
    query_grad = jnp.dot(
        wrow[:, :n_all], pall.reshape(n_data * columns, width), preferred_element_type=jnp.float32
    )
    for h in range(hard_count):
        query_grad = query_grad + wrow[:, n_all + h:n_all + h + 1].astype(
            jnp.float32
        ) * hard_rows[h].astype(jnp.float32)
    passage_grad = lax.dot_general(
        wcol.reshape(n_row, n_data, part, columns),
        qall.reshape(n_data, n_row, part, width).transpose(1, 0, 2, 3),
        (((0, 1, 2), (0, 1, 2)), ((), ())),
        preferred_element_type=jnp.float32,
    )
    return (mean_loss, query_grad.astype(jnp.bfloat16), passage_grad.astype(jnp.bfloat16))


def solution(mesh):
    in_specs = (
        P("dp", "row"),
        P("dp", "row"),
        P("dp", "row"),
        P("dp", None),
        P("dp", None),
        P("dp"),
        P(),
    )
    out_specs = (P(), P("dp", "row"), P("dp", "row"))
    return jax.shard_map(
        on_device, mesh=mesh, in_specs=in_specs, out_specs=out_specs, check_vma=False
    )
```
